32 devices in a mesh: parts: 2 (over y), col: 16 (over z, x, core).
Axes of the slice: x: 2, y: 2, z: 4, core: 2. Of those that a mesh axis runs over, the one named last changes fastest.
Arguments:
- alignment_rows: bfloat16 [128, 128, 256], P('parts', 'col'), parts along dimension 0, may hold values from -6 to 6
- alignment_columns: bfloat16 [128, 256, 256], P('parts', 'col'), parts along dimension 0, may hold values from -6 to 6
- slab_alignment_mask: int32 [128, 128], P('parts'), parts along dimension 0, may hold values 0 or 1
- slab_crop_mask: int32 [256], P('parts'), parts along dimension 0, may hold values 0 or 1
- column_alignment_mask: int32 [128, 256], P('parts', 'col'), parts along dimension 0, may hold values 0 or 1
- column_crop_mask: int32 [512], P(('parts', 'col')), parts along dimension 0, may hold values 0 or 1
- norm_scale_gain: float32 [256], replicated, may hold values from 0.25 to 1.75
- norm_offset_bias: float32 [256], replicated, may hold values from -3 to 3
- left_projection_weight: bfloat16 [256, 32], replicated, may hold values from -0.375 to 0.375
- right_projection_weight: bfloat16 [256, 32], replicated, may hold values from -0.375 to 0.375
- pair_output_weight: bfloat16 [1024, 128], replicated, may hold values from -1.5 to 1.5
- pair_output_bias: float32 [128], replicated, may hold values from -3 to 3
- pair_update_gradient: bfloat16 [256, 256, 128], P('parts', 'col'), parts along dimension 0, may hold values from -4 to 4
Outputs:
- pair_out: bfloat16 [256, 256, 128], P('parts', 'col'), parts along dimension 0
- grad_rows: bfloat16 [128, 128, 256], P('parts', 'col'), parts along dimension 0
- grad_cols: bfloat16 [128, 256, 256], P('parts', 'col'), parts along dimension 0
- grad_pair_weight: float32 [2048, 128], P(('parts', 'col')), parts along dimension 0
- grad_proj: float32 [512, 64], P(('parts', 'col')), parts along dimension 0
The draws below stay inside these ranges and needn't reach their ends.
There are 2 independent parts, one for each index of `parts`. The reference program is written for one: setup_inputs(seed, part) draws one part's arguments, and reference() takes and returns one part's arrays. A program takes and returns all parts, laid end to end along the dimension named above; an argument that names none is the same for every part. Nothing has to cross between parts.
All inputs are finite; a program needn't handle non-finite values. No bound on the sum of `column_alignment_mask` or of `column_crop_mask` on one device may be relied on, other than what follows from the above.
Results may differ from the reference program's by a relative error of at most 0.007.
Values may be sent and summed in bfloat16 or wider, within the bound.
A program may use at most 128 MiB of HBM per device.

```python
import jax
import jax.numpy as jnp
from jax import lax

ALIGNMENT_WIDTH = 256
PROJECTED_WIDTH = 32
PAIR_WIDTH = 128
ALIGNMENT_COUNT = 64
SLAB_ROW_COUNT = 128
CROP_RESIDUES = 256


def place_ends(values, stream_key, low, largest):
    longest = values.shape.index(max(values.shape))
    spots = []
    for shift in (0, 1):
        where = [jax.random.randint(jax.random.fold_in(stream_key, axis), (), 0, length) for axis, length in enumerate(values.shape)]
        where[longest] = (where[longest] + shift) % values.shape[longest]
        spots.append(tuple(where))
    return values.at[spots[0]].set(low).at[spots[1]].set(largest)


def strengthened(result, key, source, target, parts, factor):
    owner, partner = [(jnp.arange(result.shape[dim]) // (result.shape[dim] // parts)).reshape([-1 if axis == dim else 1 for axis in range(result.ndim)]) for dim in (source, target)]
    chosen = jax.random.permutation(key, parts)[partner]
    strong = (owner == chosen) | (owner == (partner + parts // 2) % parts)
    return jnp.where(strong, factor * result, result)


def steps_of(stream_key, shape, cuts, low, largest):
    def one(position, blocks):
        heights = jax.random.uniform(jax.random.fold_in(jax.random.fold_in(stream_key, 6), position), (blocks,), jnp.float32, low / len(cuts), largest / len(cuts))
        return jnp.repeat(jnp.exp(heights), shape[position] // blocks).reshape((-1,) + (1,) * (len(shape) - position - 1))

    level = one(*cuts[0])
    for cut in cuts[1:]:
        level = level * one(*cut)
    return level


def gaussian(stream_key, extent, scale, limit, cuts=(), dtype=jnp.bfloat16):
    drawn = scale * jax.random.normal(stream_key, extent, jnp.float32)
    if cuts:
        drawn = drawn * steps_of(stream_key, extent, cuts, -0.22, 0.18)
    return jnp.clip(drawn, -limit, limit).astype(dtype)


def heavy_noise(stream_key, extent, deviation, bound, shards, heavy, dtype=jnp.bfloat16):
    values = deviation * jax.random.normal(stream_key, extent, jnp.float32)
    if shards:
        values = values * steps_of(stream_key, extent, shards, -0.22, 0.18)
    return jnp.clip(strengthened(values, jax.random.fold_in(stream_key, 3), *heavy), -bound, bound).astype(dtype)


def setup_inputs(seed: int = 0, part: int = 0) -> dict:
    key_of = jax.random.split(jax.random.key(seed), 14)
    own_keys = jax.random.split(jax.random.fold_in(key_of[13], part), 14)
    alignment_rows = gaussian(own_keys[0], (ALIGNMENT_COUNT, SLAB_ROW_COUNT, ALIGNMENT_WIDTH), 1.0, 6.0, ((1, 16),))
    alignment_columns = gaussian(own_keys[1], (ALIGNMENT_COUNT, CROP_RESIDUES, ALIGNMENT_WIDTH), 1.0, 6.0, ((1, 16),))
    slab_alignment_mask = place_ends((jax.random.randint(own_keys[2], (ALIGNMENT_COUNT, SLAB_ROW_COUNT), 0, 8) < 7).astype(jnp.int32), jax.random.fold_in(own_keys[2], 1), 0, 1)
    slab_crop_mask = place_ends((jax.random.randint(own_keys[3], (SLAB_ROW_COUNT,), 0, 16) < 15).astype(jnp.int32), jax.random.fold_in(own_keys[3], 1), 0, 1)
    column_alignment_mask = place_ends((jax.random.randint(own_keys[4], (ALIGNMENT_COUNT, CROP_RESIDUES), 0, 8) < 7).astype(jnp.int32), jax.random.fold_in(own_keys[4], 1), 0, 1)
    column_crop_mask = place_ends((jax.random.randint(own_keys[5], (CROP_RESIDUES,), 0, 16) < 15).astype(jnp.int32), jax.random.fold_in(own_keys[5], 1), 0, 1)
    norm_scale_gain = jnp.clip(1.0 + 0.15 * jax.random.normal(key_of[6], (ALIGNMENT_WIDTH,), jnp.float32), 0.25, 1.75)
    norm_offset_bias = gaussian(key_of[7], (ALIGNMENT_WIDTH,), 0.5, 3.0, (), jnp.float32)
    left_projection_weight = gaussian(key_of[8], (ALIGNMENT_WIDTH, PROJECTED_WIDTH), ALIGNMENT_WIDTH ** -0.5, 0.375)
    right_projection_weight = gaussian(key_of[9], (ALIGNMENT_WIDTH, PROJECTED_WIDTH), ALIGNMENT_WIDTH ** -0.5, 0.375)
    pair_output_weight = gaussian(key_of[10], (PROJECTED_WIDTH * PROJECTED_WIDTH, PAIR_WIDTH), 0.25, 1.5)
    pair_output_bias = gaussian(key_of[11], (PAIR_WIDTH,), 0.5, 3.0, (), jnp.float32)
    pair_update_gradient = heavy_noise(own_keys[12], (SLAB_ROW_COUNT, CROP_RESIDUES, PAIR_WIDTH), 0.5, 4.0, ((1, 16),), (1, 0, 16, 2.0))
    return {"alignment_rows": alignment_rows, "alignment_columns": alignment_columns, "slab_alignment_mask": slab_alignment_mask, "slab_crop_mask": slab_crop_mask, "column_alignment_mask": column_alignment_mask, "column_crop_mask": column_crop_mask, "norm_scale_gain": norm_scale_gain, "norm_offset_bias": norm_offset_bias, "left_projection_weight": left_projection_weight, "right_projection_weight": right_projection_weight, "pair_output_weight": pair_output_weight, "pair_output_bias": pair_output_bias, "pair_update_gradient": pair_update_gradient}


norm_eps = 1e-05

def apply_layer_norm(value_array, gain, shift):
    value_array = value_array.astype(jnp.float32)
    center = value_array - lax.optimization_barrier(jnp.mean(value_array, axis=-1, keepdims=True))
    spread = lax.optimization_barrier(jnp.mean(center * center, axis=-1, keepdims=True))
    return center * lax.rsqrt(spread + norm_eps) * gain + shift

def reference(alignment_rows, alignment_columns, slab_alignment_mask, slab_crop_mask, column_alignment_mask, column_crop_mask, norm_scale_gain, norm_offset_bias, left_projection_weight, right_projection_weight, pair_output_weight, pair_output_bias, pair_update_gradient):
    row_mask_weight = (slab_alignment_mask * slab_crop_mask[None, :]).astype(jnp.float32)
    column_mask_weight = (column_alignment_mask * column_crop_mask[None, :]).astype(jnp.float32)
    normalized_rows = apply_layer_norm(alignment_rows, norm_scale_gain, norm_offset_bias).astype(jnp.bfloat16)
    normalized_columns = apply_layer_norm(alignment_columns, norm_scale_gain, norm_offset_bias).astype(jnp.bfloat16)
    left_factor = jnp.dot(normalized_rows.reshape(-1, ALIGNMENT_WIDTH), left_projection_weight, preferred_element_type=jnp.float32)
    left_factor = (left_factor.reshape(ALIGNMENT_COUNT, SLAB_ROW_COUNT, PROJECTED_WIDTH) * row_mask_weight[:, :, None]).astype(jnp.bfloat16)
    right_factor = jnp.dot(normalized_columns.reshape(-1, ALIGNMENT_WIDTH), right_projection_weight, preferred_element_type=jnp.float32)
    right_factor = (right_factor.reshape(ALIGNMENT_COUNT, CROP_RESIDUES, PROJECTED_WIDTH) * column_mask_weight[:, :, None]).astype(jnp.bfloat16)
    denom = jnp.maximum(jnp.dot(row_mask_weight.T, column_mask_weight, precision=lax.Precision.HIGHEST, preferred_element_type=jnp.float32), 1.0)
    left_expanded = left_factor.astype(jnp.float32)
    right_wide = right_factor.astype(jnp.float32)
    row_block_inputs = 16
    mask_count_total = SLAB_ROW_COUNT // row_block_inputs
    left_factor_blocks = left_expanded.reshape(ALIGNMENT_COUNT, mask_count_total, row_block_inputs, PROJECTED_WIDTH).transpose(1, 0, 2, 3)
    denom_blocks = denom.reshape(mask_count_total, row_block_inputs, CROP_RESIDUES)
    grad_blocks = pair_update_gradient.reshape(mask_count_total, row_block_inputs, CROP_RESIDUES, PAIR_WIDTH)
    weight_back = pair_output_weight.T

    def step(carry, item):
        weight_sum, right_sum = carry
        remaining_rows, rows_denom, rows_grad = item
        outer = jnp.einsum('sic,sjd->ijcd', remaining_rows, right_wide) / rows_denom[:, :, None, None]
        flat = outer.astype(jnp.bfloat16).reshape(-1, PROJECTED_WIDTH * PROJECTED_WIDTH)
        pair = (jnp.dot(flat, pair_output_weight, preferred_element_type=jnp.float32) + pair_output_bias).astype(jnp.bfloat16)
        grad_flat = rows_grad.reshape(-1, PAIR_WIDTH)
        grad_outer = (jnp.dot(grad_flat, weight_back, preferred_element_type=jnp.float32) / rows_denom.reshape(-1, 1)).astype(jnp.bfloat16)
        weight_sum = weight_sum + jnp.dot(flat.T, grad_flat, preferred_element_type=jnp.float32)
        grad_four = grad_outer.astype(jnp.float32).reshape(row_block_inputs, CROP_RESIDUES, PROJECTED_WIDTH, PROJECTED_WIDTH)
        left_part = jnp.einsum('ijcd,sjd->sic', grad_four, right_wide)
        right_sum = right_sum + jnp.einsum('ijcd,sic->sjd', grad_four, remaining_rows)
        return ((weight_sum, right_sum), (pair.reshape(row_block_inputs, CROP_RESIDUES, PAIR_WIDTH), left_part))
    start_index = (jnp.zeros((PROJECTED_WIDTH * PROJECTED_WIDTH, PAIR_WIDTH), jnp.float32), jnp.zeros((ALIGNMENT_COUNT, CROP_RESIDUES, PROJECTED_WIDTH), jnp.float32))
    (grad_pair_weight, right_sum), (pairs, left_factor_pieces) = lax.scan(step, start_index, (left_factor_blocks, denom_blocks, grad_blocks))
    pair_out = pairs.reshape(SLAB_ROW_COUNT, CROP_RESIDUES, PAIR_WIDTH)
    left_total_sum = left_factor_pieces.transpose(1, 0, 2, 3).reshape(ALIGNMENT_COUNT, SLAB_ROW_COUNT, PROJECTED_WIDTH)
    left_side_gradient = (left_total_sum * row_mask_weight[:, :, None]).astype(jnp.bfloat16)
    right_side_gradient = (right_sum * column_mask_weight[:, :, None]).astype(jnp.bfloat16)
    projected_left = jnp.dot(normalized_rows.reshape(-1, ALIGNMENT_WIDTH).T, left_side_gradient.reshape(-1, PROJECTED_WIDTH), preferred_element_type=jnp.float32)
    projected_right = jnp.dot(normalized_columns.reshape(-1, ALIGNMENT_WIDTH).T, right_side_gradient.reshape(-1, PROJECTED_WIDTH), preferred_element_type=jnp.float32)
    grad_proj = jnp.concatenate([projected_left, projected_right], axis=1)
    normalized_row_gradient = jnp.dot(left_side_gradient.reshape(-1, PROJECTED_WIDTH), left_projection_weight.T, preferred_element_type=jnp.float32).reshape(ALIGNMENT_COUNT, SLAB_ROW_COUNT, ALIGNMENT_WIDTH)
    normalized_column_gradient = jnp.dot(right_side_gradient.reshape(-1, PROJECTED_WIDTH), right_projection_weight.T, preferred_element_type=jnp.float32).reshape(ALIGNMENT_COUNT, CROP_RESIDUES, ALIGNMENT_WIDTH)
    unused_result, row_back_grads = jax.vjp(lambda value_array: apply_layer_norm(value_array, norm_scale_gain, norm_offset_bias), alignment_rows.astype(jnp.float32))
    unused_result, column_back_grads = jax.vjp(lambda value_array: apply_layer_norm(value_array, norm_scale_gain, norm_offset_bias), alignment_columns.astype(jnp.float32))
    grad_rows = row_back_grads(normalized_row_gradient)[0].astype(jnp.bfloat16)
    grad_cols = column_back_grads(normalized_column_gradient)[0].astype(jnp.bfloat16)
    return (pair_out, grad_rows, grad_cols, grad_pair_weight, grad_proj)
```

```python
import functools

import jax
import jax.numpy as jnp
from jax import lax
from jax.experimental import pallas as pl
from jax.experimental.pallas import tpu as pltpu
from jax.sharding import PartitionSpec as P

F32 = jnp.float32
BF16 = jnp.bfloat16
M = 256
C = 32
PW = 128
S = 64
NI = 128
J = 16
EPS = 1e-05
VMEM_LIMIT = 48 * 1024 * 1024

NN = (((1,), (0,)), ((), ()))
NT = (((1,), (1,)), ((), ()))
TN = (((0,), (0,)), ((), ()))


def dot(a, b, dims=NN):
    return lax.dot_general(a, b, dims, preferred_element_type=F32)


def eye(n):
    r = lax.broadcasted_iota(jnp.int32, (n, n), 0)
    c = lax.broadcasted_iota(jnp.int32, (n, n), 1)
    return (r == c).astype(F32).astype(BF16)


def turned(a):
    return dot(eye(a.shape[1]), a, NT)


def row_weights(sm_ref, sc_ref):
    return (sm_ref[...] * sc_ref[...]).astype(F32).astype(BF16)


def col_weights_t(cm_ref, cc_ref):
    return turned((cm_ref[...] * cc_ref[...]).astype(F32).astype(BF16))


def local_weights_t(rw, lr):
    pad = max(lr, 8)
    first = lax.axis_index("col") * lr
    r = lax.broadcasted_iota(jnp.int32, (pad, NI), 0) + first
    c = lax.broadcasted_iota(jnp.int32, (pad, NI), 1)
    return dot((r == c).astype(F32).astype(BF16), rw, NT)


def normalize(x):
    mean = jnp.mean(x, axis=-1, keepdims=True)
    center = x - mean
    rstd = lax.rsqrt(jnp.mean(center * center, axis=-1, keepdims=True) + EPS)
    return center * rstd, rstd


def put_halves(ref, rows, value):
    ref[0, 0:rows, :] = value[:, 0:128]
    ref[1, 0:rows, :] = value[:, 128:256]


def get_halves(ref, start, stride):
    return jnp.concatenate(
        [ref[h, pl.ds(start, S, stride), :] for h in range(2)], axis=1
    )


def project_kernel(lr, xr, xc, sm, sc, cm, cc, gain, bias, wl, wr, left, right, buf):
    rw = row_weights(sm, sc)
    lw = local_weights_t(rw, lr)
    cw = col_weights_t(cm, cc)
    for x_ref, w_ref, weights, count, out in ((xc, wr, cw, J, right), (xr, wl, lw, lr, left)):
        w_t = turned(w_ref[...]).astype(BF16)
        xhat, _ = normalize(x_ref[...].astype(F32))
        normed = (xhat * gain[...] + bias[...]).astype(BF16)
        put_halves(buf, S * count, normed.astype(F32))
        for i in range(count):
            part = get_halves(buf, i, count).astype(BF16)
            prod = dot(w_t, part, NT) * weights[i : i + 1, :]
            out[i * C : (i + 1) * C, :] = prod.astype(BF16)


def pair_kernel(
    lic, right, g, w, pbias, sm, sc, cm, cc,
    pair, gw, gl, gr,
    l32, lt, g32, gall, o, gy, p32, gl32,
):
    rw = row_weights(sm, sc)
    cw = col_weights_t(cm, cc)
    denom = jnp.maximum(dot(cw.astype(BF16), rw), 1.0)
    inv = 1.0 / denom
    l32[:, 0:S] = lic[...].astype(F32)
    g32[...] = g[...].astype(F32)
    rt = right[...]
    for c in range(C):
        lt[c * NI : (c + 1) * NI, :] = l32[pl.ds(c, NI, C), :][:, 0:S].astype(BF16)
    wv = w[...]
    for j in range(J):
        gj = g32[pl.ds(j, NI, J), :].astype(BF16)
        gall[j * NI : (j + 1) * NI, :] = gj
        go = (dot(wv, gj, NT) * inv[j : j + 1, :]).astype(BF16)
        for c in range(C):
            gy[j * C : (j + 1) * C, c * NI : (c + 1) * NI] = go[c * C : (c + 1) * C, :]
    for c in range(C):
        y = dot(rt, lt[c * NI : (c + 1) * NI, :], NT)
        for j in range(J):
            o[c * C : (c + 1) * C, j * NI : (j + 1) * NI] = (
                y[j * C : (j + 1) * C, :] * inv[j : j + 1, :]
            ).astype(BF16)
    r = turned(rt).astype(BF16)
    for c in range(C):
        part = dot(r, gy[:, c * NI : (c + 1) * NI])
        gl32[pl.ds(c, NI, C), :] = jnp.concatenate([part, part], axis=0).T
    gl[...] = gl32[:, 0:S].astype(gl.dtype)
    acc = dot(gy[...], lt[...])
    for j in range(J):
        gr[j * C : (j + 1) * C, :] = (acc[j * C : (j + 1) * C, :] * cw[j : j + 1, :]).astype(BF16)
    gw[...] = dot(o[...], gall[...])
    for j in range(J):
        pj = dot(o[:, j * NI : (j + 1) * NI], wv, TN) + pbias[...]
        p32[pl.ds(j, NI, J), :] = pj
    pair[...] = p32[...].astype(BF16)


def finish_kernel(
    n, lr, glr, gwr, gr, xr, xc, sm, sc, gain, bias, wl, wr,
    grows, gcols, gw, proj, buf, dbuf,
):
    lw = local_weights_t(row_weights(sm, sc), lr)
    gw[...] = jnp.sum(gwr[...].astype(F32), axis=0)
    total = jnp.sum(glr[...].astype(F32), axis=0)
    projs = []
    for x_ref, w_ref, count, out in ((xr, wl, lr, grows), (xc, wr, J, gcols)):
        rows = S * count
        w_t = turned(w_ref[...]).astype(BF16)
        xhat, rstd = normalize(x_ref[...].astype(F32))
        normed = (xhat * gain[...] + bias[...]).astype(BF16)
        put_halves(buf, rows, normed.astype(F32))
        acc = jnp.zeros((C, M), F32)
        for i in range(count):
            if count == J and x_ref is xc:
                gi = gr[i * C : (i + 1) * C, :]
            else:
                gi = (total[i * C : (i + 1) * C, :] * lw[i : i + 1, :]).astype(BF16)
            part = get_halves(buf, i, count).astype(BF16)
            acc = acc + dot(gi, part)
            dn = dot(turned(gi).astype(BF16), w_t)
            dbuf[0, pl.ds(i, S, count), :] = dn[:, 0:128]
            dbuf[1, pl.ds(i, S, count), :] = dn[:, 128:256]
        projs.append(acc)
        dx = jnp.concatenate([dbuf[0, 0:rows, :], dbuf[1, 0:rows, :]], axis=1) * gain[...]
        m1 = jnp.mean(dx, axis=-1, keepdims=True)
        m2 = jnp.mean(dx * xhat, axis=-1, keepdims=True)
        out[...] = ((dx - m1 - xhat * m2) * rstd).astype(BF16)
    both = jnp.concatenate(projs + projs, axis=0)
    proj[...] = both.T[:, 0 : 2 * C]


def greet(n, me):
    barrier = pltpu.get_barrier_semaphore()
    for k in range(1, n):
        pl.semaphore_signal(
            barrier, inc=1, device_id={"col": lax.rem(me + k, n)},
            device_id_type=pl.DeviceIdType.MESH,
        )
    pl.semaphore_wait(barrier, n - 1)


def exchange_kernel(n, whole, count, *refs):
    ins, outs = refs[:count], refs[count : 2 * count]
    send, recv, own = refs[2 * count :]
    me = lax.axis_index("col")
    greet(n, me)
    copies = []
    for k in range(1, n):
        peer = lax.rem(me + k, n)
        for a in range(count):
            copy = pltpu.make_async_remote_copy(
                src_ref=ins[a] if whole else ins[a].at[peer],
                dst_ref=outs[a].at[me],
                send_sem=send.at[a, k],
                recv_sem=recv.at[a, k],
                device_id={"col": peer},
                device_id_type=pl.DeviceIdType.MESH,
            )
            copy.start()
            copies.append(copy)
    for a in range(count):
        copy = pltpu.make_async_copy(ins[a] if whole else ins[a].at[me], outs[a].at[me], own.at[a])
        copy.start()
        copies.append(copy)
    for copy in copies:
        copy.wait()


def exchange(n, whole, cid, *arrays):
    count = len(arrays)
    return pl.pallas_call(
        functools.partial(exchange_kernel, n, whole, count),
        out_shape=[
            jax.ShapeDtypeStruct(((n,) + a.shape) if whole else a.shape, a.dtype) for a in arrays
        ],
        in_specs=[pl.BlockSpec(memory_space=pltpu.VMEM)] * count,
        out_specs=[pl.BlockSpec(memory_space=pltpu.VMEM)] * count,
        scratch_shapes=[
            pltpu.SemaphoreType.DMA((count, n)),
            pltpu.SemaphoreType.DMA((count, n)),
            pltpu.SemaphoreType.DMA((count,)),
        ],
        compiler_params=pltpu.CompilerParams(
            collective_id=cid, has_side_effects=True, vmem_limit_bytes=VMEM_LIMIT
        ),
        name="exchange%d" % cid,
    )(*arrays)


def call(kernel, outs, scratch, *args):
    return pl.pallas_call(
        kernel,
        out_shape=[jax.ShapeDtypeStruct(s, d) for s, d in outs],
        scratch_shapes=[pltpu.VMEM(s, d) for s, d in scratch],
        compiler_params=pltpu.CompilerParams(vmem_limit_bytes=VMEM_LIMIT),
    )(*args)


def per_device(n, xr, xc, sm, sc, cm, cc, gain, bias, wl, wr, w, pbias, g):
    lr = xr.shape[1]
    xr = xr.reshape(S * lr, M)
    xc = xc.reshape(S * J, M)
    sc, cc = sc[None, :], cc[None, :]
    gain, bias, pbias = gain[None, :], bias[None, :], pbias[None, :]
    g = g.reshape(NI * J, PW)
    left, right = call(
        functools.partial(project_kernel, lr),
        [((lr * C, S), BF16), ((J * C, S), BF16)],
        [((2, S * max(J, lr), 128), F32)],
        xr, xc, sm, sc, cm, cc, gain, bias, wl, wr,
    )
    (lic,) = exchange(n, True, 0, left)
    pair, gw, gl, gr = call(
        pair_kernel,
        [((NI * J, PW), BF16), ((C * C, PW), F32), ((NI * C, S), F32), ((J * C, S), BF16)],
        [
            ((NI * C, 128), F32), ((NI * C, S), BF16), ((NI * J, PW), F32), ((NI * J, PW), BF16),
            ((C * C, NI * J), BF16), ((J * C, NI * C), BF16), ((NI * J, PW), F32),
            ((NI * C, 128), F32),
        ],
        lic.reshape(NI * C, S), right, g, w, pbias, sm, sc, cm, cc,
    )
    glr, gwr = exchange(
        n, False, 1, gl.reshape(n, lr * C, S), gw.reshape(n, C * C // n, PW)
    )
    grows, gcols, gw, proj = call(
        functools.partial(finish_kernel, n, lr),
        [((S * lr, M), BF16), ((S * J, M), BF16), ((C * C // n, PW), F32), ((M, 2 * C), F32)],
        [((2, S * max(J, lr), 128), F32)] * 2,
        glr, gwr, gr, xr, xc, sm, sc, gain, bias, wl, wr,
    )
    (prs,) = exchange(n, False, 2, proj.reshape(n, M // n, 2 * C))
    return (
        pair.reshape(NI, J, PW),
        grows.reshape(S, lr, M),
        gcols.reshape(S, J, M),
        gw,
        jnp.sum(prs, axis=0),
    )


def solution(mesh):
    placed = (
        P("parts", "col", None), P("parts", "col", None), P("parts", None), P("parts"),
        P("parts", "col"), P(("parts", "col")), P(), P(), P(), P(), P(), P(),
        P("parts", "col", None),
    )
    return jax.shard_map(
        functools.partial(per_device, mesh.shape["col"]),
        mesh=mesh,
        in_specs=placed,
        out_specs=(
            P("parts", "col", None), P("parts", "col", None), P("parts", "col", None),
            P(("parts", "col"), None), P(("parts", "col"), None),
        ),
        check_vma=False,
    )
```

```python
import functools

import jax
import jax.numpy as jnp
from jax import lax
from jax.experimental import pallas as pl
from jax.experimental.pallas import tpu as pltpu
from jax.sharding import PartitionSpec as P

F32 = jnp.float32
BF16 = jnp.bfloat16
M = 256
C = 32
H = C // 2
PW = 128
S = 64
NI = 128
J = 16
EPS = 1e-05
VMEM_LIMIT = 48 * 1024 * 1024

NN = (((1,), (0,)), ((), ()))
NT = (((1,), (1,)), ((), ()))
TN = (((0,), (0,)), ((), ()))


def dot(a, b, dims=NN):
    return lax.dot_general(a, b, dims, preferred_element_type=F32)


def eye(n):
    r = lax.broadcasted_iota(jnp.int32, (n, n), 0)
    c = lax.broadcasted_iota(jnp.int32, (n, n), 1)
    return (r == c).astype(F32).astype(BF16)


def turned(a):
    return dot(eye(a.shape[1]), a, NT)


def row_weights(sm_ref, sc_ref):
    return (sm_ref[...] * sc_ref[...]).astype(F32).astype(BF16)


def col_weights_t(cmt_ref, cc_ref):
    crop = jnp.broadcast_to(cc_ref[...].astype(F32), (8, J)).astype(BF16)
    return cmt_ref[...].astype(F32) * turned(crop)[:, 0:1]


def local_weights_t(rw, lr):
    pad = max(lr, 8)
    first = lax.axis_index("col") * lr
    r = lax.broadcasted_iota(jnp.int32, (pad, NI), 0) + first
    c = lax.broadcasted_iota(jnp.int32, (pad, NI), 1)
    return dot((r == c).astype(F32).astype(BF16), rw, NT)


def normalize(x):
    mean = jnp.mean(x, axis=-1, keepdims=True)
    center = x - mean
    rstd = lax.rsqrt(jnp.mean(center * center, axis=-1, keepdims=True) + EPS)
    return center * rstd, rstd


def put_halves(ref, rows, value):
    ref[0, 0:rows, :] = value[:, 0:128]
    ref[1, 0:rows, :] = value[:, 128:256]


def get_halves(ref, start, stride):
    return jnp.concatenate(
        [ref[h, pl.ds(start, S, stride), :] for h in range(2)], axis=1
    )


def inverse_denom(cw, rw):
    return 1.0 / jnp.maximum(dot(cw.astype(BF16), rw), 1.0)


def first_kernel(
    lr, xr, xc, sm, sc, cmt, cc, gain, bias, wlt, wrt, g, w,
    left, right, gall, gy, gl, buf, g32, gl32,
):
    rw = row_weights(sm, sc)
    lw = local_weights_t(rw, lr)
    cw = col_weights_t(cmt, cc)
    inv = inverse_denom(cw, rw)
    for x_ref, w_ref, count in ((xc, wrt, J), (xr, wlt, lr)):
        w_t = w_ref[...]
        xhat, _ = normalize(x_ref[...].astype(F32))
        normed = (xhat * gain[...] + bias[...]).astype(BF16)
        put_halves(buf, S * count, normed.astype(F32))
        for i in range(count):
            part = get_halves(buf, i, count).astype(BF16)
            prod = dot(w_t, part, NT)
            if x_ref is xc:
                right[i * C : (i + 1) * C, :] = (prod * cw[i : i + 1, :]).astype(BF16)
            else:
                prod = prod * lw[i : i + 1, :]
                left[i * H : (i + 1) * H, :] = jnp.concatenate(
                    [prod[0:H, :], prod[H:C, :]], axis=1
                ).astype(BF16)
    g32[...] = g[...].astype(F32)
    wv = w[...]
    for j in range(J):
        gj = g32[pl.ds(j, NI, J), :].astype(BF16)
        gall[j * NI : (j + 1) * NI, :] = gj
        go = (dot(wv, gj, NT) * inv[j : j + 1, :]).astype(BF16)
        for c in range(C):
            gy[j * C : (j + 1) * C, c * NI : (c + 1) * NI] = go[c * C : (c + 1) * C, :]
    r = turned(right[...]).astype(BF16)
    for c in range(H):
        low = dot(r, gy[:, c * NI : (c + 1) * NI])
        high = dot(r, gy[:, (c + H) * NI : (c + H + 1) * NI])
        gl32[pl.ds(c, NI, H), :] = jnp.concatenate([low, high], axis=0).T
    gl[...] = gl32[...].astype(BF16)


def middle_kernel(
    n, lr, lic, glr, right, gall, gy, w, pbias, xr, xc, sm, sc, cmt, cc, gain, bias, wlt, wrt,
    pair, gw, grows, gcols, proj, l32, lt, o, p32, buf, dbuf,
):
    rw = row_weights(sm, sc)
    lw = local_weights_t(rw, lr)
    cw = col_weights_t(cmt, cc)
    inv = inverse_denom(cw, rw)
    l32[...] = lic[...].astype(F32)
    rt = right[...]
    zero = jnp.zeros_like(rt)
    rts = (jnp.concatenate([rt, zero], axis=1), jnp.concatenate([zero, rt], axis=1))
    wv = w[...]
    for c in range(H):
        lc = l32[pl.ds(c, NI, H), :].astype(BF16)
        lt[c * NI : (c + 1) * NI, :] = lc
        for h in range(2):
            y = dot(rts[h], lc, NT)
            at = (h * H + c) * C
            for j in range(J):
                o[at : at + C, j * NI : (j + 1) * NI] = (
                    y[j * C : (j + 1) * C, :] * inv[j : j + 1, :]
                ).astype(BF16)
    gw[...] = dot(o[...], gall[...]).astype(BF16)
    for j in range(J):
        pj = dot(o[:, j * NI : (j + 1) * NI], wv, TN) + pbias[...]
        p32[pl.ds(j, NI, J), :] = pj
    pair[...] = p32[...].astype(BF16)
    ltv = lt[...]
    acc_low = dot(gy[:, 0 : H * NI], ltv)
    acc_high = dot(gy[:, H * NI : C * NI], ltv)
    acc = acc_low[:, 0:S] + acc_high[:, S : 2 * S]
    total = jnp.sum(glr[...].astype(F32), axis=0)
    projs = []
    for x_ref, w_ref, count, out in ((xr, wlt, lr, grows), (xc, wrt, J, gcols)):
        rows = S * count
        w_t = w_ref[...]
        xhat, rstd = normalize(x_ref[...].astype(F32))
        normed = (xhat * gain[...] + bias[...]).astype(BF16)
        put_halves(buf, rows, normed.astype(F32))
        ptot = jnp.zeros((C, M), F32)
        for i in range(count):
            if x_ref is xc:
                gi = (acc[i * C : (i + 1) * C, :] * cw[i : i + 1, :]).astype(BF16)
            else:
                ti = total[i * H : (i + 1) * H, :]
                ti = jnp.concatenate([ti[:, 0:S], ti[:, S : 2 * S]], axis=0)
                gi = (ti * lw[i : i + 1, :]).astype(BF16)
            part = get_halves(buf, i, count).astype(BF16)
            ptot = ptot + dot(gi, part)
            dn = dot(turned(gi).astype(BF16), w_t)
            dbuf[0, pl.ds(i, S, count), :] = dn[:, 0:128]
            dbuf[1, pl.ds(i, S, count), :] = dn[:, 128:256]
        projs.append(ptot)
        dx = jnp.concatenate([dbuf[0, 0:rows, :], dbuf[1, 0:rows, :]], axis=1) * gain[...]
        m1 = jnp.mean(dx, axis=-1, keepdims=True)
        m2 = jnp.mean(dx * xhat, axis=-1, keepdims=True)
        out[...] = ((dx - m1 - xhat * m2) * rstd).astype(BF16)
    both = jnp.concatenate(projs + projs, axis=0)
    proj[...] = both.T[:, 0 : 2 * C]


def last_kernel(gwr, prs, gw, proj):
    gw[...] = jnp.sum(gwr[...].astype(F32), axis=0)
    proj[...] = jnp.sum(prs[...], axis=0)


def greet(n, me):
    barrier = pltpu.get_barrier_semaphore()
    for k in range(1, n):
        pl.semaphore_signal(
            barrier, inc=1, device_id={"col": lax.rem(me + k, n)},
            device_id_type=pl.DeviceIdType.MESH,
        )
    pl.semaphore_wait(barrier, n - 1)


def exchange_kernel(n, whole, count, *refs):
    ins, outs = refs[:count], refs[count : 2 * count]
    send, recv, own = refs[2 * count :]
    me = lax.axis_index("col")
    greet(n, me)
    copies = []
    for k in range(1, n):
        peer = lax.rem(me + k, n)
        for a in range(count):
            copy = pltpu.make_async_remote_copy(
                src_ref=ins[a] if whole[a] else ins[a].at[peer],
                dst_ref=outs[a].at[me],
                send_sem=send.at[a, k],
                recv_sem=recv.at[a, k],
                device_id={"col": peer},
                device_id_type=pl.DeviceIdType.MESH,
            )
            copy.start()
            copies.append(copy)
    for a in range(count):
        copy = pltpu.make_async_copy(
            ins[a] if whole[a] else ins[a].at[me], outs[a].at[me], own.at[a]
        )
        copy.start()
        copies.append(copy)
    for copy in copies:
        copy.wait()


def exchange(n, whole, cid, *arrays):
    count = len(arrays)
    return pl.pallas_call(
        functools.partial(exchange_kernel, n, whole, count),
        out_shape=[
            jax.ShapeDtypeStruct(((n,) + a.shape) if f else a.shape, a.dtype)
            for a, f in zip(arrays, whole)
        ],
        in_specs=[pl.BlockSpec(memory_space=pltpu.VMEM)] * count,
        out_specs=[pl.BlockSpec(memory_space=pltpu.VMEM)] * count,
        scratch_shapes=[
            pltpu.SemaphoreType.DMA((count, n)),
            pltpu.SemaphoreType.DMA((count, n)),
            pltpu.SemaphoreType.DMA((count,)),
        ],
        compiler_params=pltpu.CompilerParams(
            collective_id=cid, has_side_effects=True, vmem_limit_bytes=VMEM_LIMIT
        ),
        name="exchange%d" % cid,
    )(*arrays)


def call(kernel, outs, scratch, *args):
    return pl.pallas_call(
        kernel,
        out_shape=[jax.ShapeDtypeStruct(s, d) for s, d in outs],
        scratch_shapes=[pltpu.VMEM(s, d) for s, d in scratch],
        compiler_params=pltpu.CompilerParams(vmem_limit_bytes=VMEM_LIMIT),
    )(*args)


def per_device(n, xr, xc, sm, sc, cm, cc, gain, bias, wl, wr, w, pbias, g):
    lr = xr.shape[1]
    xr = xr.reshape(S * lr, M)
    xc = xc.reshape(S * J, M)
    sc, cc = sc[None, :], cc[None, :]
    gain, bias, pbias = gain[None, :], bias[None, :], pbias[None, :]
    g = g.reshape(NI * J, PW)
    cmt, wlt, wrt = cm.T, wl.T, wr.T
    halves = ((2, S * max(J, lr), 128), F32)
    left, right, gall, gy, gl = call(
        functools.partial(first_kernel, lr),
        [
            ((lr * H, 128), BF16), ((J * C, S), BF16), ((NI * J, PW), BF16),
            ((J * C, NI * C), BF16), ((NI * H, 128), BF16),
        ],
        [halves, ((NI * J, PW), F32), ((NI * H, 128), F32)],
        xr, xc, sm, sc, cmt, cc, gain, bias, wlt, wrt, g, w,
    )
    lic, glr = exchange(n, (True, False), 0, left, gl.reshape(n, lr * H, 128))
    pair, gw, grows, gcols, proj = call(
        functools.partial(middle_kernel, n, lr),
        [
            ((NI * J, PW), BF16), ((C * C, PW), BF16), ((S * lr, M), BF16), ((S * J, M), BF16),
            ((M, 2 * C), F32),
        ],
        [
            ((NI * H, 128), F32), ((NI * H, 128), BF16), ((C * C, NI * J), BF16),
            ((NI * J, PW), F32), halves, halves,
        ],
        lic.reshape(NI * H, 128), glr, right, gall, gy, w, pbias, xr, xc, sm, sc, cmt, cc,
        gain, bias, wlt, wrt,
    )
    gwr, prs = exchange(
        n, (False, False), 1, gw.reshape(n, C * C // n, PW), proj.reshape(n, M // n, 2 * C)
    )
    gw, proj = call(
        last_kernel, [((C * C // n, PW), F32), ((M // n, 2 * C), F32)], [], gwr, prs
    )
    return (
        pair.reshape(NI, J, PW),
        grows.reshape(S, lr, M),
        gcols.reshape(S, J, M),
        gw,
        proj,
    )


def solution(mesh):
    placed = (
        P("parts", "col", None), P("parts", "col", None), P("parts", None), P("parts"),
        P("parts", "col"), P(("parts", "col")), P(), P(), P(), P(), P(), P(),
        P("parts", "col", None),
    )
    return jax.shard_map(
        functools.partial(per_device, mesh.shape["col"]),
        mesh=mesh,
        in_specs=placed,
        out_specs=(
            P("parts", "col", None), P("parts", "col", None), P("parts", "col", None),
            P(("parts", "col"), None), P(("parts", "col"), None),
        ),
        check_vma=False,
    )
```

```python
import functools

import jax
import jax.numpy as jnp
from jax import lax
from jax.experimental import pallas as pl
from jax.experimental.pallas import tpu as pltpu
from jax.sharding import PartitionSpec as P

F32 = jnp.float32
BF16 = jnp.bfloat16
M = 256
C = 32
H = C // 2
PW = 128
S = 64
NI = 128
J = 16
EPS = 1e-05
VMEM_LIMIT = 63 * 1024 * 1024

NN = (((1,), (0,)), ((), ()))
NT = (((1,), (1,)), ((), ()))
TN = (((0,), (0,)), ((), ()))


def dot(a, b, dims=NN):
    return lax.dot_general(a, b, dims, preferred_element_type=F32)


def eye(n):
    r = lax.broadcasted_iota(jnp.int32, (n, n), 0)
    c = lax.broadcasted_iota(jnp.int32, (n, n), 1)
    return (r == c).astype(F32).astype(BF16)


def turned(a):
    return dot(eye(a.shape[1]), a, NT)


def row_weights(sm_ref, sc_ref):
    return (sm_ref[...] * sc_ref[...]).astype(F32).astype(BF16)


def col_weights_t(cmt_ref, cc_ref):
    crop = jnp.broadcast_to(cc_ref[...].astype(F32), (8, J)).astype(BF16)
    return cmt_ref[...].astype(F32) * turned(crop)[:, 0:1]


def local_weights_t(rw, lr):
    pad = max(lr, 8)
    first = lax.axis_index("col") * lr
    r = lax.broadcasted_iota(jnp.int32, (pad, NI), 0) + first
    c = lax.broadcasted_iota(jnp.int32, (pad, NI), 1)
    return dot((r == c).astype(F32).astype(BF16), rw, NT)


def normalize(x):
    mean = jnp.mean(x, axis=-1, keepdims=True)
    center = x - mean
    rstd = lax.rsqrt(jnp.mean(center * center, axis=-1, keepdims=True) + EPS)
    return center * rstd, rstd


def put_halves(ref, rows, value):
    ref[0, 0:rows, :] = value[:, 0:128]
    ref[1, 0:rows, :] = value[:, 128:256]


def get_halves(ref, start, stride):
    return jnp.concatenate(
        [ref[h, pl.ds(start, S, stride), :] for h in range(2)], axis=1
    )


def inverse_denom(cw, rw):
    return 1.0 / jnp.maximum(dot(cw.astype(BF16), rw), 1.0)


def lanes(ref, i, j):
    return jnp.concatenate([ref[i], ref[j]], axis=1)


def body(n, lr, *refs):
    hbm, refs = refs[:COUNT], refs[COUNT:]
    (pair, grows, gcols, gw, proj), refs = refs[:5], refs[5:]
    ins, refs = refs[:COUNT], refs[COUNT:]
    (
        left, lic, gls, glr, gws, gwr, prs, prr, right, gall, gy, o, lt, l32, g32, gl32, p32,
        bufr, bufc, xhr, xhc, rsr, rsc, dbr, dbc, in_sem, send, recv,
    ) = refs
    xr, xc, sm, sc, cmt, cc, gain, bias, wlt, wrt, w, pbias, g = ins
    me = lax.axis_index("col")
    barrier = pltpu.get_barrier_semaphore()
    for k in range(1, n):
        pl.semaphore_signal(
            barrier, inc=1, device_id={"col": lax.rem(me + k, n)},
            device_id_type=pl.DeviceIdType.MESH,
        )
    loads = [pltpu.make_async_copy(hbm[i], ins[i], in_sem.at[i]) for i in range(COUNT)]
    for copy in loads:
        copy.start()

    def exchange(a, src, dst, whole):
        copies = []
        for k in range(1, n):
            peer = lax.rem(me + k, n)
            copy = pltpu.make_async_remote_copy(
                src_ref=src if whole else src.at[peer],
                dst_ref=dst.at[me],
                send_sem=send.at[a, k],
                recv_sem=recv.at[a, k],
                device_id={"col": peer},
                device_id_type=pl.DeviceIdType.MESH,
            )
            copy.start()
            copies.append(copy)
        dst[me] = src[...] if whole else src[me]
        return copies

    for i in (2, 3, 4, 5, 6, 7, 8, 9, 0):
        loads[i].wait()
    rw = row_weights(sm, sc)
    lw = local_weights_t(rw, lr)
    cw = col_weights_t(cmt, cc)
    inv = inverse_denom(cw, rw)

    def norm(x_ref, count, xh, rs, buf):
        xhat, rstd = normalize(x_ref[...].astype(F32))
        xh[...] = xhat
        rs[...] = rstd
        normed = (xhat * gain[...] + bias[...]).astype(BF16)
        put_halves(buf, S * count, normed.astype(F32))

    norm(xr, lr, xhr, rsr, bufr)
    for i in range(lr):
        prod = dot(wlt[...], get_halves(bufr, i, lr).astype(BF16), NT) * lw[i : i + 1, :]
        left[i * H : (i + 1) * H, :] = jnp.concatenate(
            [prod[0:H, :], prod[H:C, :]], axis=1
        ).astype(BF16)
    pl.semaphore_wait(barrier, n - 1)
    gather = exchange(0, left, lic, True)

    loads[1].wait()
    norm(xc, J, xhc, rsc, bufc)
    for j in range(J):
        prod = dot(wrt[...], get_halves(bufc, j, J).astype(BF16), NT)
        right[j * C : (j + 1) * C, :] = (prod * cw[j : j + 1, :]).astype(BF16)
    for i in (10, 11, 12):
        loads[i].wait()
    g32[...] = g[...].astype(F32)
    wv = w[...]
    for j in range(J):
        gj = g32[pl.ds(j, NI, J), :].astype(BF16)
        gall[j * NI : (j + 1) * NI, :] = gj
        go = (dot(wv, gj, NT) * inv[j : j + 1, :]).astype(BF16)
        gy[:, j * C : (j + 1) * C, :] = go.reshape(C, C, NI)
    rt = right[...]
    r = turned(rt).astype(BF16)
    for c in range(H):
        both = jnp.concatenate([dot(r, gy[c]), dot(r, gy[c + H])], axis=0)
        gl32[pl.ds(c, NI, H), :] = both.T
    gls[...] = gl32[...].astype(BF16).reshape(n, lr * H, 128)
    lefts = exchange(1, gls, glr, False)

    for copy in gather:
        copy.wait_recv()
    l32[...] = lic[...].astype(F32).reshape(NI * H, 128)
    zero = jnp.zeros_like(rt)
    rts = (jnp.concatenate([rt, zero], axis=1), jnp.concatenate([zero, rt], axis=1))
    inv3 = inv[:, None, :]
    for c in range(H):
        lc = l32[pl.ds(c, NI, H), :].astype(BF16)
        lt[c * NI : (c + 1) * NI, :] = lc
        for h in range(2):
            y = dot(rts[h], lc, NT)
            at = (h * H + c) * C
            o[:, at : at + C, :] = (y.reshape(J, C, NI) * inv3).astype(BF16)
    acc = jnp.zeros((C * C, PW), F32)
    for j in range(0, J, 2):
        acc = acc + dot(lanes(o, j, j + 1), gall[j * NI : (j + 2) * NI, :])
    gws[...] = acc.astype(BF16).reshape(n, C * C // n, PW)
    weights = exchange(2, gws, gwr, False)

    halves = []
    for h in range(2):
        acc = jnp.zeros((J * C, 2 * S), F32)
        for c in range(0, H, 2):
            acc = acc + dot(lanes(gy, h * H + c, h * H + c + 1), lt[c * NI : (c + 2) * NI, :])
        halves.append(acc[:, h * S : (h + 1) * S])
    racc = halves[0] + halves[1]

    def back(count, grad, weights_t, buf, w_ref, db):
        ptot = jnp.zeros((C, M), F32)
        for i in range(count):
            gi = (grad(i) * weights_t[i : i + 1, :]).astype(BF16)
            ptot = ptot + dot(gi, get_halves(buf, i, count).astype(BF16))
            dn = dot(turned(gi).astype(BF16), w_ref[...])
            db[0, pl.ds(i, S, count), :] = dn[:, 0:128]
            db[1, pl.ds(i, S, count), :] = dn[:, 128:256]
        return ptot

    def norm_back(out, db, xh, rs):
        dx = jnp.concatenate([db[0], db[1]], axis=1) * gain[...]
        xhat = xh[...]
        m1 = jnp.mean(dx, axis=-1, keepdims=True)
        m2 = jnp.mean(dx * xhat, axis=-1, keepdims=True)
        out[...] = ((dx - m1 - xhat * m2) * rs[...]).astype(BF16)

    pright = back(J, lambda i: racc[i * C : (i + 1) * C, :], cw, bufc, wrt, dbc)
    for copy in lefts:
        copy.wait_recv()
    total = jnp.sum(glr[...].astype(F32), axis=0)

    def left_grad(i):
        ti = total[i * H : (i + 1) * H, :]
        return jnp.concatenate([ti[:, 0:S], ti[:, S : 2 * S]], axis=0)

    pleft = back(lr, left_grad, lw, bufr, wlt, dbr)
    stacked = jnp.concatenate([pleft, pright, pleft, pright], axis=0)
    prs[...] = stacked.T[:, 0 : 2 * C].reshape(n, M // n, 2 * C)
    projs = exchange(3, prs, prr, False)

    for j in range(J):
        p32[pl.ds(j, NI, J), :] = dot(o[j], wv, TN) + pbias[...]
    pair[...] = p32[...].astype(BF16)
    norm_back(grows, dbr, xhr, rsr)
    norm_back(gcols, dbc, xhc, rsc)
    for copy in weights:
        copy.wait_recv()
    gw[...] = jnp.sum(gwr[...].astype(F32), axis=0)
    for copy in projs:
        copy.wait_recv()
    proj[...] = jnp.sum(prr[...], axis=0)
    for copy in gather + lefts + weights + projs:
        copy.wait_send()


COUNT = 13


def per_device(n, xr, xc, sm, sc, cm, cc, gain, bias, wl, wr, w, pbias, g):
    lr = xr.shape[1]
    args = (
        xr.reshape(S * lr, M), xc.reshape(S * J, M), sm, sc[None, :], cm.T, cc[None, :],
        gain[None, :], bias[None, :], wl.T, wr.T, w, pbias[None, :], g.reshape(NI * J, PW),
    )
    vmem = pltpu.VMEM
    part = C * C // n
    pair, grows, gcols, gw, proj = pl.pallas_call(
        functools.partial(body, n, lr),
        out_shape=[
            jax.ShapeDtypeStruct((NI * J, PW), BF16),
            jax.ShapeDtypeStruct((S * lr, M), BF16),
            jax.ShapeDtypeStruct((S * J, M), BF16),
            jax.ShapeDtypeStruct((part, PW), F32),
            jax.ShapeDtypeStruct((M // n, 2 * C), F32),
        ],
        in_specs=[pl.BlockSpec(memory_space=pltpu.HBM)] * COUNT,
        out_specs=[pl.BlockSpec(memory_space=pltpu.VMEM)] * 5,
        scratch_shapes=[vmem(a.shape, a.dtype) for a in args]
        + [
            vmem((lr * H, 128), BF16), vmem((n, lr * H, 128), BF16),
            vmem((n, lr * H, 128), BF16), vmem((n, lr * H, 128), BF16),
            vmem((n, part, PW), BF16), vmem((n, part, PW), BF16),
            vmem((n, M // n, 2 * C), F32), vmem((n, M // n, 2 * C), F32),
            vmem((J * C, S), BF16), vmem((NI * J, PW), BF16),
            vmem((C, J * C, NI), BF16), vmem((J, C * C, NI), BF16), vmem((NI * H, 128), BF16),
            vmem((NI * H, 128), F32), vmem((NI * J, PW), F32), vmem((NI * H, 128), F32),
            vmem((NI * J, PW), F32),
            vmem((2, S * lr, 128), F32), vmem((2, S * J, 128), F32),
            vmem((S * lr, M), F32), vmem((S * J, M), F32),
            vmem((S * lr, 1), F32), vmem((S * J, 1), F32),
            vmem((2, S * lr, 128), F32), vmem((2, S * J, 128), F32),
            pltpu.SemaphoreType.DMA((COUNT,)),
            pltpu.SemaphoreType.DMA((4, n)), pltpu.SemaphoreType.DMA((4, n)),
        ],
        compiler_params=pltpu.CompilerParams(
            collective_id=0, has_side_effects=True, vmem_limit_bytes=VMEM_LIMIT
        ),
        name="outer_product_mean",
    )(*args)
    return (
        pair.reshape(NI, J, PW),
        grows.reshape(S, lr, M),
        gcols.reshape(S, J, M),
        gw,
        proj,
    )


def solution(mesh):
    placed = (
        P("parts", "col", None), P("parts", "col", None), P("parts", None), P("parts"),
        P("parts", "col"), P(("parts", "col")), P(), P(), P(), P(), P(), P(),
        P("parts", "col", None),
    )
    return jax.shard_map(
        functools.partial(per_device, mesh.shape["col"]),
        mesh=mesh,
        in_specs=placed,
        out_specs=(
            P("parts", "col", None), P("parts", "col", None), P("parts", "col", None),
            P(("parts", "col"), None), P(("parts", "col"), None),
        ),
        check_vma=False,
    )
```

```python
import functools

import jax
import jax.numpy as jnp
from jax import lax
from jax.experimental import pallas as pl
from jax.experimental.pallas import tpu as pltpu
from jax.sharding import PartitionSpec as P

F32 = jnp.float32
BF16 = jnp.bfloat16
M = 256
C = 32
H = C // 2
PW = 128
S = 64
NI = 128
J = 16
EPS = 1e-05
VMEM_LIMIT = 63 * 1024 * 1024

NN = (((1,), (0,)), ((), ()))
NT = (((1,), (1,)), ((), ()))
TN = (((0,), (0,)), ((), ()))


def dot(a, b, dims=NN):
    return lax.dot_general(a, b, dims, preferred_element_type=F32)


def eye(n):
    r = lax.broadcasted_iota(jnp.int32, (n, n), 0)
    c = lax.broadcasted_iota(jnp.int32, (n, n), 1)
    return (r == c).astype(F32).astype(BF16)


def turned(a):
    return dot(eye(a.shape[1]), a, NT)


def row_weights(sm_ref, sc_ref):
    return (sm_ref[...] * sc_ref[...]).astype(F32).astype(BF16)


def col_weights_t(cmt_ref, cc_ref):
    crop = jnp.broadcast_to(cc_ref[...].astype(F32), (8, J)).astype(BF16)
    return cmt_ref[...].astype(F32) * turned(crop)[:, 0:1]


def local_weights_t(rw, lr):
    pad = max(lr, 8)
    first = lax.axis_index("col") * lr
    r = lax.broadcasted_iota(jnp.int32, (pad, NI), 0) + first
    c = lax.broadcasted_iota(jnp.int32, (pad, NI), 1)
    return dot((r == c).astype(F32).astype(BF16), rw, NT)


def normalize(x):
    mean = jnp.mean(x, axis=-1, keepdims=True)
    center = x - mean
    rstd = lax.rsqrt(jnp.mean(center * center, axis=-1, keepdims=True) + EPS)
    return center * rstd, rstd


def put_halves(ref, rows, value):
    ref[0, 0:rows, :] = value[:, 0:128]
    ref[1, 0:rows, :] = value[:, 128:256]


def get_halves(ref, start, stride):
    return jnp.concatenate(
        [ref[h, pl.ds(start, S, stride), :] for h in range(2)], axis=1
    )


def inverse_denom(cw, rw):
    return 1.0 / jnp.maximum(dot(cw.astype(BF16), rw), 1.0)


def lanes(ref, i, j):
    return jnp.concatenate([ref[i], ref[j]], axis=1)


def body(n, lr, *refs):
    hbm, refs = refs[:COUNT], refs[COUNT:]
    (pair, grows, gcols, gw, proj), refs = refs[:5], refs[5:]
    ins, refs = refs[:COUNT], refs[COUNT:]
    (
        left, lic, gls, glr, gws, gwr, prs, prr, right, gall, gy, o, lt, l32, g32, gl32, p32,
        bufr, bufc, xhr, xhc, rsr, rsc, dbr, dbc, in_sem, send, recv,
    ) = refs
    xr, xc, sm, sc, cmt, cc, gain, bias, wlt, wrt, w, pbias, g = ins
    me = lax.axis_index("col")
    barrier = pltpu.get_barrier_semaphore()
    for k in range(1, n):
        pl.semaphore_signal(
            barrier, inc=1, device_id={"col": lax.rem(me + k, n)},
            device_id_type=pl.DeviceIdType.MESH,
        )
    loads = [pltpu.make_async_copy(hbm[i], ins[i], in_sem.at[i]) for i in range(COUNT)]
    for copy in loads:
        copy.start()

    def exchange(a, src, dst, whole):
        copies = []
        for k in range(1, n):
            peer = lax.rem(me + k, n)
            copy = pltpu.make_async_remote_copy(
                src_ref=src if whole else src.at[peer],
                dst_ref=dst.at[me],
                send_sem=send.at[a, k],
                recv_sem=recv.at[a, k],
                device_id={"col": peer},
                device_id_type=pl.DeviceIdType.MESH,
            )
            copy.start()
            copies.append(copy)
        dst[me] = src[...] if whole else src[me]
        return copies

    for i in (2, 3, 4, 5, 6, 7, 8, 9, 0):
        loads[i].wait()
    rw = row_weights(sm, sc)
    lw = local_weights_t(rw, lr)
    cw = col_weights_t(cmt, cc)
    inv = inverse_denom(cw, rw)

    def norm(x_ref, count, xh, rs, buf):
        xhat, rstd = normalize(x_ref[...].astype(F32))
        xh[...] = xhat
        rs[...] = rstd
        normed = (xhat * gain[...] + bias[...]).astype(BF16)
        put_halves(buf, S * count, normed.astype(F32))

    norm(xr, lr, xhr, rsr, bufr)
    for i in range(lr):
        prod = dot(wlt[...], get_halves(bufr, i, lr).astype(BF16), NT) * lw[i : i + 1, :]
        left[i * H : (i + 1) * H, :] = jnp.concatenate(
            [prod[0:H, :], prod[H:C, :]], axis=1
        ).astype(BF16)
    pl.semaphore_wait(barrier, n - 1)
    half = n // 2
    other = me + 1 - 2 * lax.rem(me, 2)

    def pass_on(k, src, at, peer):
        copy = pltpu.make_async_remote_copy(
            src_ref=src,
            dst_ref=lic.at[at],
            send_sem=send.at[0, k],
            recv_sem=recv.at[0, k],
            device_id={"col": peer},
            device_id_type=pl.DeviceIdType.MESH,
        )
        copy.start()
        return copy

    direct = [pass_on(k, left, me, lax.rem(me + 2 * k, n)) for k in range(1, half)]
    gather = [pass_on(0, left, me, other)]
    lic[me] = left[...]

    loads[1].wait()
    norm(xc, J, xhc, rsc, bufc)
    for j in range(J):
        prod = dot(wrt[...], get_halves(bufc, j, J).astype(BF16), NT)
        right[j * C : (j + 1) * C, :] = (prod * cw[j : j + 1, :]).astype(BF16)
    for i in (10, 11, 12):
        loads[i].wait()
    g32[...] = g[...].astype(F32)
    wv = w[...]
    for j in range(J):
        gj = g32[pl.ds(j, NI, J), :].astype(BF16)
        gall[j * NI : (j + 1) * NI, :] = gj
        go = (dot(wv, gj, NT) * inv[j : j + 1, :]).astype(BF16)
        gy[:, j * C : (j + 1) * C, :] = go.reshape(C, C, NI)
    rt = right[...]
    r = turned(rt).astype(BF16)
    for c in range(H):
        both = jnp.concatenate([dot(r, gy[c]), dot(r, gy[c + H])], axis=0)
        gl32[pl.ds(c, NI, H), :] = both.T
    gls[...] = gl32[...].astype(BF16).reshape(n, lr * H, 128)
    lefts = exchange(1, gls, glr, False)

    for k in range(1, half):
        direct[k - 1].wait_recv()
        at = lax.rem(me - 2 * k + n, n)
        gather.append(pass_on(half + k, lic.at[at], at, other))
    for copy in gather:
        copy.wait_recv()
    l32[...] = lic[...].astype(F32).reshape(NI * H, 128)
    zero = jnp.zeros_like(rt)
    rts = (jnp.concatenate([rt, zero], axis=1), jnp.concatenate([zero, rt], axis=1))
    inv3 = inv[:, None, :]
    for c in range(H):
        lc = l32[pl.ds(c, NI, H), :].astype(BF16)
        lt[c * NI : (c + 1) * NI, :] = lc
        for h in range(2):
            y = dot(rts[h], lc, NT)
            at = (h * H + c) * C
            o[:, at : at + C, :] = (y.reshape(J, C, NI) * inv3).astype(BF16)
    acc = jnp.zeros((C * C, PW), F32)
    for j in range(0, J, 2):
        acc = acc + dot(lanes(o, j, j + 1), gall[j * NI : (j + 2) * NI, :])
    gws[...] = acc.astype(BF16).reshape(n, C * C // n, PW)
    weights = exchange(2, gws, gwr, False)

    halves = []
    for h in range(2):
        acc = jnp.zeros((J * C, 2 * S), F32)
        for c in range(0, H, 2):
            acc = acc + dot(lanes(gy, h * H + c, h * H + c + 1), lt[c * NI : (c + 2) * NI, :])
        halves.append(acc[:, h * S : (h + 1) * S])
    racc = halves[0] + halves[1]

    def back(count, grad, weights_t, buf, w_ref, db):
        ptot = jnp.zeros((C, M), F32)
        for i in range(count):
            gi = (grad(i) * weights_t[i : i + 1, :]).astype(BF16)
            ptot = ptot + dot(gi, get_halves(buf, i, count).astype(BF16))
            dn = dot(turned(gi).astype(BF16), w_ref[...])
            db[0, pl.ds(i, S, count), :] = dn[:, 0:128]
            db[1, pl.ds(i, S, count), :] = dn[:, 128:256]
        return ptot

    def norm_back(out, db, xh, rs):
        dx = jnp.concatenate([db[0], db[1]], axis=1) * gain[...]
        xhat = xh[...]
        m1 = jnp.mean(dx, axis=-1, keepdims=True)
        m2 = jnp.mean(dx * xhat, axis=-1, keepdims=True)
        out[...] = ((dx - m1 - xhat * m2) * rs[...]).astype(BF16)

    pright = back(J, lambda i: racc[i * C : (i + 1) * C, :], cw, bufc, wrt, dbc)
    for copy in lefts:
        copy.wait_recv()
    total = jnp.sum(glr[...].astype(F32), axis=0)

    def left_grad(i):
        ti = total[i * H : (i + 1) * H, :]
        return jnp.concatenate([ti[:, 0:S], ti[:, S : 2 * S]], axis=0)

    pleft = back(lr, left_grad, lw, bufr, wlt, dbr)
    stacked = jnp.concatenate([pleft, pright, pleft, pright], axis=0)
    prs[...] = stacked.T[:, 0 : 2 * C].reshape(n, M // n, 2 * C)
    projs = exchange(3, prs, prr, False)

    for j in range(J):
        p32[pl.ds(j, NI, J), :] = dot(o[j], wv, TN) + pbias[...]
    pair[...] = p32[...].astype(BF16)
    norm_back(grows, dbr, xhr, rsr)
    norm_back(gcols, dbc, xhc, rsc)
    for copy in weights:
        copy.wait_recv()
    gw[...] = jnp.sum(gwr[...].astype(F32), axis=0)
    for copy in projs:
        copy.wait_recv()
    proj[...] = jnp.sum(prr[...], axis=0)
    for copy in direct + gather + lefts + weights + projs:
        copy.wait_send()


COUNT = 13


def per_device(n, xr, xc, sm, sc, cm, cc, gain, bias, wl, wr, w, pbias, g):
    lr = xr.shape[1]
    args = (
        xr.reshape(S * lr, M), xc.reshape(S * J, M), sm, sc[None, :], cm.T, cc[None, :],
        gain[None, :], bias[None, :], wl.T, wr.T, w, pbias[None, :], g.reshape(NI * J, PW),
    )
    vmem = pltpu.VMEM
    part = C * C // n
    pair, grows, gcols, gw, proj = pl.pallas_call(
        functools.partial(body, n, lr),
        out_shape=[
            jax.ShapeDtypeStruct((NI * J, PW), BF16),
            jax.ShapeDtypeStruct((S * lr, M), BF16),
            jax.ShapeDtypeStruct((S * J, M), BF16),
            jax.ShapeDtypeStruct((part, PW), F32),
            jax.ShapeDtypeStruct((M // n, 2 * C), F32),
        ],
        in_specs=[pl.BlockSpec(memory_space=pltpu.HBM)] * COUNT,
        out_specs=[pl.BlockSpec(memory_space=pltpu.VMEM)] * 5,
        scratch_shapes=[vmem(a.shape, a.dtype) for a in args]
        + [
            vmem((lr * H, 128), BF16), vmem((n, lr * H, 128), BF16),
            vmem((n, lr * H, 128), BF16), vmem((n, lr * H, 128), BF16),
            vmem((n, part, PW), BF16), vmem((n, part, PW), BF16),
            vmem((n, M // n, 2 * C), F32), vmem((n, M // n, 2 * C), F32),
            vmem((J * C, S), BF16), vmem((NI * J, PW), BF16),
            vmem((C, J * C, NI), BF16), vmem((J, C * C, NI), BF16), vmem((NI * H, 128), BF16),
            vmem((NI * H, 128), F32), vmem((NI * J, PW), F32), vmem((NI * H, 128), F32),
            vmem((NI * J, PW), F32),
            vmem((2, S * lr, 128), F32), vmem((2, S * J, 128), F32),
            vmem((S * lr, M), F32), vmem((S * J, M), F32),
            vmem((S * lr, 1), F32), vmem((S * J, 1), F32),
            vmem((2, S * lr, 128), F32), vmem((2, S * J, 128), F32),
            pltpu.SemaphoreType.DMA((COUNT,)),
            pltpu.SemaphoreType.DMA((4, n)), pltpu.SemaphoreType.DMA((4, n)),
        ],
        compiler_params=pltpu.CompilerParams(
            collective_id=0, has_side_effects=True, vmem_limit_bytes=VMEM_LIMIT
        ),
        name="outer_product_mean",
    )(*args)
    return (
        pair.reshape(NI, J, PW),
        grows.reshape(S, lr, M),
        gcols.reshape(S, J, M),
        gw,
        proj,
    )


def solution(mesh):
    placed = (
        P("parts", "col", None), P("parts", "col", None), P("parts", None), P("parts"),
        P("parts", "col"), P(("parts", "col")), P(), P(), P(), P(), P(), P(),
        P("parts", "col", None),
    )
    return jax.shard_map(
        functools.partial(per_device, mesh.shape["col"]),
        mesh=mesh,
        in_specs=placed,
        out_specs=(
            P("parts", "col", None), P("parts", "col", None), P("parts", "col", None),
            P(("parts", "col"), None), P(("parts", "col"), None),
        ),
        check_vma=False,
    )
```
